32 devices in a mesh: wide: 16 (over z, y, x), narrow: 2 (over core).
Axes of the slice: x: 2, y: 2, z: 4, core: 2. Of those that a mesh axis runs over, the one named last changes fastest.
Arguments:
- latent_tokens: float32 [384, 16384], P('narrow', 'wide'), may hold values from -52 to 52
- labels: int32 [64], P('wide'), may hold values from 0 to 1000
- timesteps: int32 [64], P('wide'), may hold values from 0 to 999
- class_table: bfloat16 [1001, 384], replicated, may hold values from -6 to 6
- modulation_weight: bfloat16 [384, 6, 384], P('wide', None, 'narrow'), may hold values from -0.3125 to 0.3125
- modulation_bias: float32 [6, 384], P(None, 'narrow'), may hold values from -3 to 3
- in_weight: bfloat16 [384, 3, 384], P('wide', None, 'narrow'), may hold values from -0.21875 to 0.21875
- in_bias: float32 [2, 384], P(None, 'narrow'), may hold values from -3 to 3
- out_weight: bfloat16 [384, 384], P('narrow', 'wide'), may hold values from -1.25 to 1.25
- out_bias: float32 [384], P('narrow'), may hold values from -3 to 3
- up_weight: bfloat16 [384, 1536], P('wide', 'narrow'), may hold values from -0.3125 to 0.3125
- up_bias: float32 [1536], P('narrow'), may hold values from -3 to 3
- down_weight: bfloat16 [1536, 384], P('narrow', 'wide'), may hold values from -0.3125 to 0.3125
- down_bias: float32 [384], P('narrow'), may hold values from -3 to 3
- cotangent: float32 [384, 16384], P('narrow', 'wide'), may hold values from -6 to 6
Outputs:
- block_output: float32 [384, 16384], P('narrow', 'wide')
- token_grads: float32 [384, 16384], P('narrow', 'wide')
- condition_grads: float32 [64, 384], P('wide')
- table_grads: float32 [1001, 384], replicated
- modulation_grads: float32 [384, 6, 384], P('wide', None, 'narrow')
- modulation_bias_grads: float32 [6, 384], P(None, 'narrow')
- in_grads: float32 [384, 3, 384], P('wide', None, 'narrow')
- in_bias_grads: float32 [2, 384], P(None, 'narrow')
- out_grads: float32 [384, 384], P('narrow', 'wide')
- out_bias_grads: float32 [384], P('narrow')
- up_grads: float32 [384, 1536], P('wide', 'narrow')
- up_bias_grads: float32 [1536], P('narrow')
- down_grads: float32 [1536, 384], P('narrow', 'wide')
- down_bias_grads: float32 [384], P('narrow')
The draws below stay inside these ranges and needn't reach their ends.
All inputs are finite; a program needn't handle non-finite values.
Results may differ from the reference program's by a relative error of at most 0.017.
Values may be sent and summed in bfloat16 or wider, within the bound.
A program may use at most 128 MiB of HBM per device.

```python
import math
import jax
import jax.numpy as jnp
from jax import lax

D = 384
H = 6
HD = 64
FF = 1536
SEQ = 256
NCLS = 1001
NSTEPS = 1000
LATENTS = 64
TOKENS = 16384


def draw_latent_tokens(key, part):
    noise_key, column_key, row_key = jax.random.split(key, 3)
    position = jnp.arange(D, dtype=jnp.float32) / (D - 1)
    column_scale = jnp.exp(math.log(4.0) * position + jax.random.uniform(column_key, (D,), jnp.float32, math.log(0.5), math.log(1.5)))
    noise = jnp.clip(jax.random.normal(noise_key, (TOKENS, D), jnp.float32), -4.0, 4.0)
    row_scale = jnp.exp(jax.random.uniform(row_key, (TOKENS, 1), jnp.float32, 0.0, math.log(10.0)))
    return jnp.transpose(noise * row_scale * column_scale[None, :] * 0.15)


def plant(drawn, own_key, smallest, high):
    shape = drawn.shape
    spot = [jax.random.randint(jax.random.fold_in(own_key, axis), (), 0, shape[axis]) for axis in range(len(shape))]
    drawn = drawn.at[tuple(spot)].set(smallest)
    longest = shape.index(max(shape))
    spot[longest] = (spot[longest] + 1) % shape[longest]
    return drawn.at[tuple(spot)].set(high)


def with_spikes(values, key, source, target, shards_of, factor):
    owner, partner = [(jnp.arange(values.shape[dim]) // (values.shape[dim] // shards_of)).reshape([-1 if axis == dim else 1 for axis in range(values.ndim)]) for dim in (source, target)]
    chosen = jax.random.permutation(key, shards_of)[partner]
    strong = (owner == chosen) | (owner == (partner + shards_of // 2) % shards_of)
    return jnp.where(strong, factor * values, values)


def block_levels(rng, extent, cuts, least, largest):
    level = 1.0
    for dim, blocks in cuts:
        draws = jax.random.uniform(jax.random.fold_in(jax.random.fold_in(rng, 6), dim), (blocks,), jnp.float32, least / len(cuts), largest / len(cuts))
        level = level * jnp.repeat(jnp.exp(draws), extent[dim] // blocks).reshape((-1,) + (1,) * (len(extent) - 1 - dim))
    return level


def normal_values(stream_key, shape, scale, most, shards=(), kind=jnp.bfloat16):
    values = jax.random.normal(stream_key, shape, jnp.float32) * scale
    if len(shards) > 0:
        values = block_levels(stream_key, shape, shards, -0.22, 0.18) * values
    return jnp.clip(values, min=-most, max=most).astype(kind)


def bell_draw_with(own_key, shape, deviation, reach, cuts, heavy, held_as=jnp.bfloat16):
    drawn = deviation * jax.random.normal(own_key, shape, jnp.float32)
    if cuts:
        drawn = drawn * block_levels(own_key, shape, cuts, -0.22, 0.18)
    return jnp.clip(with_spikes(drawn, jax.random.fold_in(own_key, 3), *heavy), -reach, reach).astype(held_as)


def setup_inputs(seed: int = 0) -> dict:
    key_list = jax.random.split(jax.random.key(seed), 16)
    return {
        "latent_tokens": draw_latent_tokens(jax.random.fold_in(key_list[15], 71), 0),
        "labels": plant(jax.random.randint(key_list[1], (LATENTS,), 0, NCLS), jax.random.fold_in(key_list[1], 1), 0, NCLS - 1).astype(jnp.int32),
        "timesteps": plant(jax.random.randint(key_list[2], (LATENTS,), 0, NSTEPS), jax.random.fold_in(key_list[2], 1), 0, NSTEPS - 1).astype(jnp.int32),
        "class_table": normal_values(key_list[3], (NCLS, D), 1.0, 6.0),
        "modulation_weight": normal_values(key_list[4], (D, 6, D), D ** -0.5, 0.3125, ((0, 16), (2, 2))),
        "modulation_bias": normal_values(key_list[5], (6, D), 0.5, 3.0, ((1, 2),), jnp.float32),
        "in_weight": normal_values(key_list[6], (D, 3, D), (2 * D) ** -0.5, 0.21875, ((0, 16), (2, 2))),
        "in_bias": normal_values(key_list[7], (2, D), 0.5, 3.0, ((1, 2),), jnp.float32),
        "out_weight": normal_values(key_list[8], (D, D), (D // 16) ** -0.5, 1.25, ((0, 2), (1, 16))),
        "out_bias": normal_values(key_list[9], (D,), 0.5, 3.0, ((0, 2),), jnp.float32),
        "up_weight": normal_values(key_list[10], (D, FF), D ** -0.5, 0.3125, ((0, 16), (1, 2))),
        "up_bias": normal_values(key_list[11], (FF,), 0.5, 3.0, ((0, 2),), jnp.float32),
        "down_weight": normal_values(key_list[12], (FF, D), (FF // 4) ** -0.5, 0.3125, ((0, 2), (1, 16))),
        "down_bias": normal_values(key_list[13], (D,), 0.5, 3.0, ((0, 2),), jnp.float32),
        "cotangent": bell_draw_with(key_list[14], (D, TOKENS), 1.0, 6.0, ((0, 2), (1, 16)), (1, 0, 16, 2.0), jnp.float32),
    }


EPS = 1e-06
GELU_K = 0.7978845608028654
GELU_A = 0.044715

def widen(array):
    return array.astype(jnp.float32)

def time_features(timesteps):
    half_width = D // 2
    frequencies = jnp.exp(jnp.arange(half_width, dtype=jnp.float32) * (-math.log(10000.0) / half_width))
    angles = timesteps.astype(jnp.float32)[:, None] * frequencies[None, :]
    return jnp.concatenate([jnp.cos(angles), jnp.sin(angles)], axis=1)

def gelu_value(inputs):
    inner = GELU_K * (inputs + GELU_A * inputs * inputs * inputs)
    return 0.5 * inputs * (1.0 + jnp.tanh(inner))

def gelu_slope(inputs):
    inner = GELU_K * (inputs + GELU_A * inputs * inputs * inputs)
    tangent = jnp.tanh(inner)
    return 0.5 * (1.0 + tangent) + 0.5 * inputs * (1.0 - tangent * tangent) * GELU_K * (1.0 + 3.0 * GELU_A * inputs * inputs)

def silu_slope(inputs):
    sigmoid = jax.nn.sigmoid(inputs)
    return sigmoid * (1.0 + inputs * (1.0 - sigmoid))

def norm_rows(values):
    centre = values - lax.optimization_barrier(jnp.mean(values, axis=-1, keepdims=True))
    inv_std = lax.rsqrt(lax.optimization_barrier(jnp.mean(centre * centre, axis=-1, keepdims=True)) + EPS)
    return (centre * inv_std, inv_std)

def norm_back(grad_norm, normed, inv_std):
    return inv_std * (grad_norm - lax.optimization_barrier(jnp.mean(grad_norm, axis=-1, keepdims=True)) - normed * lax.optimization_barrier(jnp.mean(grad_norm * normed, axis=-1, keepdims=True)))

def modulate_back(grad_mod, normed, scale):
    return (lax.optimization_barrier(jnp.sum(grad_mod, axis=1)), lax.optimization_barrier(jnp.sum(grad_mod * normed, axis=1)), grad_mod * (1.0 + scale))

def forward_backward(params, inputs):
    class_table, modulation_weight, modulation_bias, in_weight, in_bias, out_weight, out_bias, up_weight, up_bias, down_weight, down_bias = params
    tokens_in, cotangent, labels, timesteps = inputs
    latent_count = labels.shape[0]
    hidden_in = tokens_in.reshape(latent_count, SEQ, D)
    upstream = cotangent.reshape(latent_count, SEQ, D)
    head_shape = (latent_count, SEQ, H, HD)
    score_scale = HD ** (-0.5)
    condition = widen(class_table[labels]) + time_features(timesteps)
    activated = jax.nn.silu(condition).astype(jnp.bfloat16)
    modulation = jnp.einsum('bd,djf->bjf', widen(activated), widen(modulation_weight)) + modulation_bias
    shift_one, scale_one, gate_one, shift_two, scale_two, gate_two = [modulation[:, which][:, None, :] for which in range(6)]
    normed_one, inv_one = norm_rows(hidden_in)
    modulated_one = (normed_one * (1.0 + scale_one) + shift_one).astype(jnp.bfloat16)
    projected = jnp.einsum('bsd,djf->bsjf', widen(modulated_one), widen(in_weight))
    queries = (projected[:, :, 0] + in_bias[0]).astype(jnp.bfloat16).reshape(head_shape)
    key_rows = projected[:, :, 1].astype(jnp.bfloat16).reshape(head_shape)
    value_rows = (projected[:, :, 2] + in_bias[1]).astype(jnp.bfloat16).reshape(head_shape)
    scores = jnp.einsum('bshe,bthe->bhst', widen(queries), widen(key_rows)) * score_scale
    log_total = jnp.log(lax.optimization_barrier(jnp.sum(jnp.exp(scores), axis=-1, keepdims=True)))
    mixing = jnp.exp(scores - log_total).astype(jnp.bfloat16)
    attended = jnp.einsum('bhst,bthe->bshe', widen(mixing), widen(value_rows)).astype(jnp.bfloat16).reshape(latent_count, SEQ, D)
    attention = jnp.einsum('bsd,de->bse', widen(attended), widen(out_weight)) + out_bias
    middle = hidden_in + gate_one * attention
    normed_two, inv_two = norm_rows(middle)
    modulated_two = (normed_two * (1.0 + scale_two) + shift_two).astype(jnp.bfloat16)
    pre_act = jnp.einsum('bsd,df->bsf', widen(modulated_two), widen(up_weight)) + up_bias
    activation = gelu_value(pre_act).astype(jnp.bfloat16)
    feedforward = jnp.einsum('bsf,fd->bsd', widen(activation), widen(down_weight)) + down_bias
    block_output = middle + gate_two * feedforward
    gate_two_grad = lax.optimization_barrier(jnp.sum(upstream * feedforward, axis=1))
    grad_ff = gate_two * upstream
    grad_ff_bf = grad_ff.astype(jnp.bfloat16)
    down_total = jnp.einsum('bsf,bsd->fd', widen(activation), widen(grad_ff_bf))
    grad_pre = jnp.einsum('bsd,fd->bsf', widen(grad_ff_bf), widen(down_weight)) * gelu_slope(pre_act)
    grad_pre_bf = grad_pre.astype(jnp.bfloat16)
    up_total = jnp.einsum('bsd,bsf->df', widen(modulated_two), widen(grad_pre_bf))
    grad_mod_two = jnp.einsum('bsf,df->bsd', widen(grad_pre_bf), widen(up_weight))
    shift_two_grad, scale_two_grad, grad_norm_two = modulate_back(grad_mod_two, normed_two, scale_two)
    grad_middle = upstream + norm_back(grad_norm_two, normed_two, inv_two)
    gate_one_grad = lax.optimization_barrier(jnp.sum(grad_middle * attention, axis=1))
    grad_att = gate_one * grad_middle
    grad_att_bf = grad_att.astype(jnp.bfloat16)
    out_total = jnp.einsum('bsd,bse->de', widen(attended), widen(grad_att_bf))
    grad_attended = jnp.einsum('bse,de->bsd', widen(grad_att_bf), widen(out_weight)).astype(jnp.bfloat16).reshape(head_shape)
    weights_full = jnp.exp(scores - log_total)
    grad_mixing = jnp.einsum('bshe,bthe->bhst', widen(grad_attended), widen(value_rows))
    row_dots = lax.optimization_barrier(jnp.sum(weights_full * grad_mixing, axis=-1, keepdims=True))
    grad_scores = (weights_full * (grad_mixing - row_dots) * score_scale).astype(jnp.bfloat16)
    grad_queries = jnp.einsum('bhst,bthe->bshe', widen(grad_scores), widen(key_rows)).reshape(latent_count, SEQ, D)
    grad_keys = jnp.einsum('bhst,bshe->bthe', widen(grad_scores), widen(queries)).reshape(latent_count, SEQ, D)
    grad_values = jnp.einsum('bhst,bshe->bthe', widen(mixing), widen(grad_attended)).reshape(latent_count, SEQ, D)
    grad_proj = jnp.stack([grad_queries, grad_keys, grad_values], axis=2).astype(jnp.bfloat16)
    in_total = jnp.einsum('bsd,bsjf->djf', widen(modulated_one), widen(grad_proj))
    grad_mod_one = jnp.einsum('bsjf,djf->bsd', widen(grad_proj), widen(in_weight))
    shift_one_grad, scale_one_grad, grad_norm_one = modulate_back(grad_mod_one, normed_one, scale_one)
    token_grads = grad_middle + norm_back(grad_norm_one, normed_one, inv_one)
    grad_modulation = jnp.stack([shift_one_grad, scale_one_grad, gate_one_grad, shift_two_grad, scale_two_grad, gate_two_grad], axis=1)
    grad_modulation_bf = grad_modulation.astype(jnp.bfloat16)
    modulation_total = jnp.einsum('bd,bjf->djf', widen(activated), widen(grad_modulation_bf))
    grad_activated = jnp.einsum('bjf,djf->bd', widen(grad_modulation_bf), widen(modulation_weight))
    condition_grads = grad_activated * silu_slope(condition) * SEQ ** (-0.5)
    table_part = jax.ops.segment_sum(condition_grads, labels, num_segments=NCLS)
    in_bias_part = jnp.stack([lax.optimization_barrier(jnp.sum(grad_queries, axis=(0, 1))), lax.optimization_barrier(jnp.sum(grad_values, axis=(0, 1)))])
    grads = (table_part, modulation_total, lax.optimization_barrier(jnp.sum(grad_modulation, axis=0)), in_total, in_bias_part, out_total, lax.optimization_barrier(jnp.sum(grad_att, axis=(0, 1))), up_total, lax.optimization_barrier(jnp.sum(grad_pre, axis=(0, 1))), down_total, lax.optimization_barrier(jnp.sum(grad_ff, axis=(0, 1))))
    outputs = (block_output.reshape(-1, D), token_grads.reshape(-1, D), condition_grads)
    return (outputs, grads)

def reference(latent_tokens, labels, timesteps, class_table, modulation_weight, modulation_bias, in_weight, in_bias, out_weight, out_bias, up_weight, up_bias, down_weight, down_bias, cotangent):
    block_size = math.gcd(LATENTS, 16)
    steps_count = LATENTS // block_size
    params = (class_table, modulation_weight, modulation_bias, in_weight, in_bias, out_weight, out_bias, up_weight, up_bias, down_weight, down_bias)
    token_rows = jnp.transpose(latent_tokens)
    upstream_rows = jnp.transpose(cotangent)
    inputs = (token_rows.reshape(steps_count, block_size * SEQ, D), upstream_rows.reshape(steps_count, block_size * SEQ, D), labels.reshape(steps_count, block_size).astype(jnp.int32), timesteps.reshape(steps_count, block_size).astype(jnp.int32))
    zero_grads = (jnp.zeros((NCLS, D), jnp.float32), jnp.zeros((D, 6, D), jnp.float32), jnp.zeros((6, D), jnp.float32), jnp.zeros((D, 3, D), jnp.float32), jnp.zeros((2, D), jnp.float32), jnp.zeros((D, D), jnp.float32), jnp.zeros((D,), jnp.float32), jnp.zeros((D, FF), jnp.float32), jnp.zeros((FF,), jnp.float32), jnp.zeros((FF, D), jnp.float32), jnp.zeros((D,), jnp.float32))

    def step_block(totals, piece):
        outputs, grads = forward_backward(params, piece)
        return (jax.tree.map(jnp.add, totals, grads), outputs)
    totals, stacked = lax.scan(step_block, zero_grads, inputs)
    weight_scale = TOKENS ** (-0.5)
    block_output = jnp.transpose(stacked[0].reshape(TOKENS, D))
    token_grads = jnp.transpose(stacked[1].reshape(TOKENS, D))
    condition_grads = stacked[2].reshape(LATENTS, D)
    return (block_output, token_grads, condition_grads, totals[0], totals[1] * weight_scale, totals[2] * weight_scale, totals[3] * weight_scale, totals[4] * weight_scale, totals[5] * weight_scale, totals[6] * weight_scale, totals[7] * weight_scale, totals[8] * weight_scale, totals[9] * weight_scale, totals[10] * weight_scale)
```

```python
import functools
import math

import jax
import jax.numpy as jnp
from jax import lax
from jax.experimental import pallas as pl
from jax.experimental.pallas import tpu as pltpu
from jax.sharding import PartitionSpec as P

D = 384
HD = 64
LANES = 128
MESH = pl.DeviceIdType.MESH
VMEM_LIMIT = 60 * 1024 * 1024


EPS = 1e-06
GELU_K = 0.7978845608028654
GELU_A = 0.044715


def time_features(timesteps):
    half_width = D // 2
    frequencies = jnp.exp(
        jnp.arange(half_width, dtype=jnp.float32) * (-math.log(10000.0) / half_width)
    )
    angles = timesteps.astype(jnp.float32)[:, None] * frequencies[None, :]
    return jnp.concatenate([jnp.cos(angles), jnp.sin(angles)], axis=1)


def gelu_value(inputs):
    inner = GELU_K * (inputs + GELU_A * inputs * inputs * inputs)
    return 0.5 * inputs * (1.0 + jnp.tanh(inner))


def gelu_slope(inputs):
    inner = GELU_K * (inputs + GELU_A * inputs * inputs * inputs)
    tangent = jnp.tanh(inner)
    return 0.5 * (1.0 + tangent) + 0.5 * inputs * (1.0 - tangent * tangent) * GELU_K * (
        1.0 + 3.0 * GELU_A * inputs * inputs
    )


def silu_slope(inputs):
    sigmoid = jax.nn.sigmoid(inputs)
    return sigmoid * (1.0 + inputs * (1.0 - sigmoid))


def plane(wide):
    side = max(1, round((wide / 2) ** (1 / 3)))
    while wide % (side * side):
        side -= 1
    return wide // (side * side), side


class Place:
    def __init__(self, wide):
        self.deep, self.side = plane(wide)
        self.me = lax.axis_index("wide")
        self.core = lax.axis_index("narrow")
        self.z = self.me // (self.side * self.side)
        rest = self.me % (self.side * self.side)
        major, minor = rest // self.side, rest % self.side
        self.p = major + self.core * (minor - major)
        self.q = minor + self.core * (major - minor)
        self.p_stride = self.side + self.core * (1 - self.side)
        self.q_stride = 1 + self.core * (self.side - 1)

    def index(self, dz, dp, dq):
        return (
            ((self.z + dz) % self.deep) * (self.side * self.side)
            + ((self.p + dp) % self.side) * self.p_stride
            + ((self.q + dq) % self.side) * self.q_stride
        )

    def line_peers(self):
        return (
            [self.index(dz, 0, 0) for dz in range(1, self.deep)]
            + [self.index(0, dp, 0) for dp in range(1, self.side)]
            + [self.index(0, 0, dq) for dq in range(1, self.side)]
        )


def gather_kernel(
    wide, shard, tokens, upstream, biases,
    full, tokens_out, upstream_out, biases_out,
    send, recv, pair_send, pair_recv, swap_send, swap_recv, local,
):
    at = Place(wide)
    core, other = at.core, 1 - at.core
    barrier = pltpu.get_barrier_semaphore()
    peers = at.line_peers()
    for peer in peers:
        pl.semaphore_signal(barrier, 1, device_id=(peer, core), device_id_type=MESH)
    pl.semaphore_signal(barrier, 1, device_id=(at.me, other), device_id_type=MESH)
    pl.semaphore_wait(barrier, len(peers) + 1)
    waits = []
    count = 0

    def push(src, block, target):
        nonlocal count
        copy = pltpu.make_async_remote_copy(
            src, full.at[core, block], send.at[count], recv.at[block],
            device_id=(target, core), device_id_type=MESH,
        )
        copy.start()
        waits.append(copy)
        count += 1

    def share(src, block):
        copy = pltpu.make_async_remote_copy(
            src, full.at[core, block], pair_send.at[block], pair_recv.at[block],
            device_id=(at.me, other), device_id_type=MESH,
        )
        copy.start()
        waits.append(copy)

    def arrived(block):
        pltpu.make_async_copy(full.at[core, block], full.at[core, block], recv.at[block]).wait()

    for dz in range(1, at.deep):
        push(shard, at.me, at.index(dz, 0, 0))
    for dp in range(1, at.side):
        push(shard, at.me, at.index(0, dp, 0))
    for dq in range(1, at.side):
        push(shard, at.me, at.index(0, 0, dq))
    share(shard, at.me)
    half = tokens_out.shape[2]
    mine = pl.ds(pl.multiple_of(core * half, LANES), half)
    theirs = pl.ds(pl.multiple_of(other * half, LANES), half)
    for which, (src, dst) in enumerate(
        [(tokens.at[:, theirs], tokens_out), (upstream.at[:, theirs], upstream_out), (biases, biases_out)]
    ):
        copy = pltpu.make_async_remote_copy(
            src, dst.at[core], swap_send.at[which], swap_recv.at[which],
            device_id=(at.me, other), device_id_type=MESH,
        )
        copy.start()
        waits.append(copy)
    keeps = [
        pltpu.make_async_copy(src, dst, local.at[which])
        for which, (src, dst) in enumerate(
            [
                (tokens.at[:, mine], tokens_out.at[core]),
                (upstream.at[:, mine], upstream_out.at[core]),
                (biases, biases_out.at[core]),
                (shard, full.at[core, at.me]),
            ]
        )
    ]
    for keep in keeps:
        keep.start()
    for dz in range(1, at.deep):
        block = at.index(dz, 0, 0)
        arrived(block)
        for dp in range(1, at.side):
            push(full.at[core, block], block, at.index(0, dp, 0))
        for dq in range(1, at.side):
            push(full.at[core, block], block, at.index(0, 0, dq))
        share(full.at[core, block], block)
    for dz in range(at.deep):
        for dp in range(1, at.side):
            block = at.index(dz, dp, 0)
            arrived(block)
            for dq in range(1, at.side):
                push(full.at[core, block], block, at.index(0, 0, dq))
            share(full.at[core, block], block)
    for dz in range(at.deep):
        for dq in range(1, at.side):
            for dp in range(at.side):
                block = at.index(dz, dp, dq)
                arrived(block)
                share(full.at[core, block], block)
    for keep in keeps:
        keep.wait()
    for copy in waits:
        copy.wait_send()
    for block in range(wide):
        pltpu.make_async_copy(full.at[core, block], full.at[core, block], pair_recv.at[block]).wait()
    for which, (src, dst) in enumerate(
        [(tokens_out.at[core], None), (upstream_out.at[core], None), (biases_out.at[core], None)]
    ):
        pltpu.make_async_copy(src, src, swap_recv.at[which]).wait()


def gather_all(wide, shard, tokens, upstream, biases):
    rows, columns = shard.shape
    features, count = tokens.shape
    deep, side = plane(wide)
    sends = wide * (deep + 2 * side)
    vmem = pl.BlockSpec(memory_space=pltpu.VMEM)
    return pl.pallas_call(
        functools.partial(gather_kernel, wide),
        name="gather",
        out_shape=(
            jax.ShapeDtypeStruct((2, wide, rows, columns), shard.dtype),
            jax.ShapeDtypeStruct((2, features, count // 2), tokens.dtype),
            jax.ShapeDtypeStruct((2, features, count // 2), tokens.dtype),
            jax.ShapeDtypeStruct((2,) + biases.shape, biases.dtype),
        ),
        in_specs=[vmem] * 4,
        out_specs=(vmem,) * 4,
        scratch_shapes=[
            pltpu.SemaphoreType.DMA((sends,)),
            pltpu.SemaphoreType.DMA((wide,)),
            pltpu.SemaphoreType.DMA((wide,)),
            pltpu.SemaphoreType.DMA((wide,)),
            pltpu.SemaphoreType.DMA((3,)),
            pltpu.SemaphoreType.DMA((3,)),
            pltpu.SemaphoreType.DMA((4,)),
        ],
        compiler_params=pltpu.CompilerParams(
            collective_id=0, has_side_effects=True, vmem_limit_bytes=VMEM_LIMIT
        ),
    )(shard, tokens, upstream, biases)


def scatter_kernel(
    wide, parts, message, block_out, token_out,
    total, messages, block_half, token_half,
    from_pair, from_q, from_p, from_z, sums,
    send, pair_send, pair_recv, q_recv, p_recv, z_recv,
    note_send, note_recv, swap_send, swap_recv, local,
):
    at = Place(wide)
    core, other = at.core, 1 - at.core
    barrier = pltpu.get_barrier_semaphore()
    for step in range(wide):
        peer = (at.me + step) % wide
        if step:
            pl.semaphore_signal(barrier, 1, device_id=(peer, core), device_id_type=MESH)
        pl.semaphore_signal(barrier, 1, device_id=(peer, other), device_id_type=MESH)
    pl.semaphore_wait(barrier, 2 * wide - 1)
    waits = []

    deep, side = at.deep, at.side
    order = (
        [(dz, dp, dq) for dq in range(1, side) for dp in range(side) for dz in range(deep)]
        + [(dz, dp, 0) for dp in range(1, side) for dz in range(deep)]
        + [(dz, 0, 0) for dz in range(1, deep)]
        + [(0, 0, 0)]
    )
    for dz, dp, dq in order:
        block = at.index(dz, dp, dq)
        copy = pltpu.make_async_remote_copy(
            parts.at[other, block], from_pair.at[block], pair_send.at[block], pair_recv.at[block],
            device_id=(at.me, other), device_id_type=MESH,
        )
        copy.start()
        waits.append(copy)
    for step in range(wide):
        peer = (at.me + step) % wide
        for flip in range(2):
            if step == 0 and flip == 0:
                continue
            seat = core if flip == 0 else other
            copy = pltpu.make_async_remote_copy(
                message.at[seat], messages.at[at.me, core],
                note_send.at[step, flip], note_recv.at[at.me, core],
                device_id=(peer, seat), device_id_type=MESH,
            )
            copy.start()
            waits.append(copy)
    half = block_out.shape[0] // 2
    span = block_out.shape[1]
    columns = pl.ds(pl.multiple_of(core * span, LANES), span)
    mine = pl.ds(pl.multiple_of(core * half, 8), half)
    theirs = pl.ds(pl.multiple_of(other * half, 8), half)
    keeps = [pltpu.make_async_copy(message.at[core], messages.at[at.me, core], local.at[2])]
    for which, (src, dst) in enumerate([(block_out, block_half), (token_out, token_half)]):
        copy = pltpu.make_async_remote_copy(
            src.at[theirs], dst.at[:, columns], swap_send.at[which], swap_recv.at[which],
            device_id=(at.me, other), device_id_type=MESH,
        )
        copy.start()
        waits.append(copy)
        keeps.append(pltpu.make_async_copy(src.at[mine], dst.at[:, columns], local.at[which]))
    for keep in keeps:
        keep.start()

    def landed(ref, sem):
        pltpu.make_async_copy(ref, ref, sem).wait()

    f32 = jnp.float32
    for number, (dz, dp, dq) in enumerate(order):
        block = at.index(dz, dp, dq)
        landed(from_pair.at[block], pair_recv.at[block])
        value = parts[core, block].astype(f32) + from_pair[block].astype(f32)
        zs, ps = (at.z + dz) % deep, (at.p + dp) % side
        if dq == 0:
            for s in range(side - 1):
                landed(from_q.at[s, zs, ps], q_recv.at[s, zs, ps])
                value += from_q[s, zs, ps].astype(f32)
            if dp == 0:
                for s in range(side - 1):
                    landed(from_p.at[s, zs], p_recv.at[s, zs])
                    value += from_p[s, zs].astype(f32)
        if dq:
            target, slot, sem = (
                at.index(0, 0, dq), from_q.at[side - 1 - dq, zs, ps], q_recv.at[side - 1 - dq, zs, ps]
            )
        elif dp:
            target, slot, sem = (
                at.index(0, dp, 0), from_p.at[side - 1 - dp, zs], p_recv.at[side - 1 - dp, zs]
            )
        elif dz:
            target, slot, sem = at.index(dz, 0, 0), from_z.at[deep - 1 - dz], z_recv.at[deep - 1 - dz]
        else:
            for s in range(deep - 1):
                landed(from_z.at[s], z_recv.at[s])
                value += from_z[s].astype(f32)
            total[...] = value
            continue
        sums[block] = value.astype(jnp.bfloat16)
        copy = pltpu.make_async_remote_copy(
            sums.at[block], slot, send.at[number], sem,
            device_id=(target, core), device_id_type=MESH,
        )
        copy.start()
        waits.append(copy)
    for keep in keeps:
        keep.wait()
    for copy in waits:
        copy.wait_send()
    for step in range(wide):
        peer = (at.me + step) % wide
        if step:
            landed(messages.at[peer, core], note_recv.at[peer, core])
        landed(messages.at[peer, other], note_recv.at[peer, other])
    spare = pl.ds(pl.multiple_of(other * span, LANES), span)
    landed(block_half.at[:, spare], swap_recv.at[0])
    landed(token_half.at[:, spare], swap_recv.at[1])


def scatter_all(wide, parts, message, block_out, token_out):
    rows, columns = parts.shape[2:]
    features, count = block_out.shape
    deep, side = plane(wide)
    vmem = pl.BlockSpec(memory_space=pltpu.VMEM)
    bf, f32 = jnp.bfloat16, jnp.float32
    dma = pltpu.SemaphoreType.DMA
    return pl.pallas_call(
        functools.partial(scatter_kernel, wide),
        name="scatter",
        out_shape=(
            jax.ShapeDtypeStruct((rows, columns), f32),
            jax.ShapeDtypeStruct((wide,) + message.shape, bf),
            jax.ShapeDtypeStruct((features // 2, 2 * count), f32),
            jax.ShapeDtypeStruct((features // 2, 2 * count), f32),
        ),
        in_specs=[vmem] * 4,
        out_specs=(vmem,) * 4,
        scratch_shapes=[
            pltpu.VMEM((wide, rows, columns), bf),
            pltpu.VMEM((max(side - 1, 1), deep, side, rows, columns), bf),
            pltpu.VMEM((max(side - 1, 1), deep, rows, columns), bf),
            pltpu.VMEM((max(deep - 1, 1), rows, columns), bf),
            pltpu.VMEM((wide, rows, columns), bf),
            dma((wide,)),
            dma((wide,)),
            dma((wide,)),
            dma((max(side - 1, 1), deep, side)),
            dma((max(side - 1, 1), deep)),
            dma((max(deep - 1, 1),)),
            dma((wide, 2)),
            dma((wide, 2)),
            dma((2,)),
            dma((2,)),
            dma((3,)),
        ],
        compiler_params=pltpu.CompilerParams(
            collective_id=1, has_side_effects=True, vmem_limit_bytes=VMEM_LIMIT
        ),
    )(parts, message, block_out, token_out)


def norm_forward(values):
    average = jnp.mean(values, axis=-1, keepdims=True)
    centred = values - average
    inv_std = lax.rsqrt(jnp.mean(centred * centred, axis=-1, keepdims=True) + EPS)
    return centred * inv_std, inv_std


def norm_backward(grad_norm, normed, inv_std):
    first = jnp.mean(grad_norm, axis=-1, keepdims=True)
    second = jnp.mean(grad_norm * normed, axis=-1, keepdims=True)
    return inv_std * (grad_norm - first - normed * second)


def block_pass(
    tokens, upstream, full, modulation, bias_in, bias_out, bias_up, bias_down, own, sequence, width, hidden
):
    bf, f32 = jnp.bfloat16, jnp.float32
    features = 2 * width
    score_scale = HD ** (-0.5)
    join = lambda halves: jnp.concatenate([halves[0], halves[1]], axis=-1)
    up_full = join(full[:, :, :hidden])
    down_full = join(full[:, :, hidden : 2 * hidden])
    in_full = full[:, :, 2 * hidden : 2 * hidden + 3 * width].reshape(2, features, 3, width)
    out_full = join(full[:, :, 2 * hidden + 3 * width : 2 * hidden + 4 * width])
    in_full = jnp.transpose(in_full, (1, 2, 0, 3)).reshape(features, 3, features)
    in_bias = join(bias_in.reshape(2, 2, width))
    out_bias, up_bias, down_bias = join(bias_out), join(bias_up), join(bias_down)
    hidden_in = jnp.transpose(tokens).reshape(own, sequence, features)
    up_grad = jnp.transpose(upstream).reshape(own, sequence, features)
    shift_one, scale_one, gate_one, shift_two, scale_two, gate_two = [
        modulation[:, which][:, None, :] for which in range(6)
    ]
    head_shape = (own, sequence, features // HD, HD)
    dot = functools.partial(jnp.einsum, preferred_element_type=f32)
    normed_one, inv_one = norm_forward(hidden_in)
    modulated_one = (normed_one * (1.0 + scale_one) + shift_one).astype(bf)
    projected = dot("bsd,djf->bsjf", modulated_one, in_full)
    queries = (projected[:, :, 0] + in_bias[0]).astype(bf).reshape(head_shape)
    key_rows = projected[:, :, 1].astype(bf).reshape(head_shape)
    value_rows = (projected[:, :, 2] + in_bias[1]).astype(bf).reshape(head_shape)
    scores = dot("bshe,bthe->bhst", queries, key_rows) * score_scale
    log_total = jnp.log(jnp.sum(jnp.exp(scores), axis=-1, keepdims=True))
    weights_full = jnp.exp(scores - log_total)
    mixing = weights_full.astype(bf)
    attended = dot("bhst,bthe->bshe", mixing, value_rows).astype(bf).reshape(own, sequence, features)
    attention = dot("bsd,ed->bse", attended, out_full) + out_bias
    middle = hidden_in + gate_one * attention
    normed_two, inv_two = norm_forward(middle)
    modulated_two = (normed_two * (1.0 + scale_two) + shift_two).astype(bf)
    pre_act = dot("bsd,df->bsf", modulated_two, up_full) + up_bias
    activation = gelu_value(pre_act).astype(bf)
    feedforward = dot("bsf,df->bsd", activation, down_full) + down_bias
    block_output = middle + gate_two * feedforward
    gate_two_grad = jnp.sum(up_grad * feedforward, axis=1)
    grad_ff = gate_two * up_grad
    grad_ff_bf = grad_ff.astype(bf)
    down_total = dot("bsd,bsf->df", grad_ff_bf, activation)
    grad_pre = dot("bsd,df->bsf", grad_ff_bf, down_full) * gelu_slope(pre_act)
    grad_pre_bf = grad_pre.astype(bf)
    up_total = dot("bsd,bsf->df", modulated_two, grad_pre_bf)
    grad_mod_two = dot("bsf,df->bsd", grad_pre_bf, up_full)
    shift_two_grad = jnp.sum(grad_mod_two, axis=1)
    scale_two_grad = jnp.sum(grad_mod_two * normed_two, axis=1)
    grad_middle = up_grad + norm_backward(grad_mod_two * (1.0 + scale_two), normed_two, inv_two)
    gate_one_grad = jnp.sum(grad_middle * attention, axis=1)
    grad_att = gate_one * grad_middle
    grad_att_bf = grad_att.astype(bf)
    out_total = dot("bse,bsd->ed", grad_att_bf, attended)
    grad_attended = dot("bse,ed->bsd", grad_att_bf, out_full).astype(bf).reshape(head_shape)
    grad_mixing = dot("bshe,bthe->bhst", grad_attended, value_rows)
    row_dots = jnp.sum(weights_full * grad_mixing, axis=-1, keepdims=True)
    grad_scores = (weights_full * (grad_mixing - row_dots) * score_scale).astype(bf)
    flat_shape = (own, sequence, features)
    grad_queries = dot("bhst,bthe->bshe", grad_scores, key_rows).reshape(flat_shape)
    grad_keys = dot("bhst,bshe->bthe", grad_scores, queries).reshape(flat_shape)
    grad_values = dot("bhst,bshe->bthe", mixing, grad_attended).reshape(flat_shape)
    grad_proj = jnp.stack([grad_queries, grad_keys, grad_values], axis=2).astype(bf)
    in_total = dot("bsd,bsjf->djf", modulated_one, grad_proj)
    grad_mod_one = dot("bsjf,djf->bsd", grad_proj, in_full)
    shift_one_grad = jnp.sum(grad_mod_one, axis=1)
    scale_one_grad = jnp.sum(grad_mod_one * normed_one, axis=1)
    token_grads = grad_middle + norm_backward(grad_mod_one * (1.0 + scale_one), normed_one, inv_one)
    grad_modulation = jnp.stack(
        [shift_one_grad, scale_one_grad, gate_one_grad, shift_two_grad, scale_two_grad, gate_two_grad],
        axis=1,
    )
    split = lambda value: value.astype(bf).reshape(value.shape[:-1] + (2, value.shape[-1] // 2))
    parts = [
        jnp.concatenate(
            [
                split(up_total)[:, n],
                split(down_total)[:, n],
                split(in_total)[:, :, n].reshape(features, -1),
                split(out_total)[:, n],
            ],
            axis=1,
        )
        for n in range(2)
    ]
    sums = [
        jnp.sum(grad_queries, axis=(0, 1)),
        jnp.sum(grad_values, axis=(0, 1)),
        jnp.sum(grad_att, axis=(0, 1)),
        jnp.sum(grad_pre, axis=(0, 1)),
        jnp.sum(grad_ff, axis=(0, 1)),
    ]
    bias_sums = jnp.concatenate([s.reshape(2, -1) for s in sums], axis=1)
    transposed = lambda value: jnp.transpose(value.reshape(-1, features))
    return transposed(block_output), transposed(token_grads), jnp.stack(parts), grad_modulation, bias_sums


def codes(values):
    return jnp.concatenate([values // 256, values % 256]).astype(jnp.bfloat16)


def shards(
    latent_tokens,
    labels,
    timesteps,
    class_table,
    modulation_weight,
    modulation_bias,
    in_weight,
    in_bias,
    out_weight,
    out_bias,
    up_weight,
    up_bias,
    down_weight,
    down_bias,
    cotangent,
):
    bf, f32 = jnp.bfloat16, jnp.float32
    wide = lax.axis_size("wide")
    me, core = lax.axis_index("wide"), lax.axis_index("narrow")
    latent_count = labels.shape[0]
    own = latent_count // 2
    width = latent_tokens.shape[0]
    hidden = up_weight.shape[1]
    local_tokens = latent_tokens.shape[1]
    sequence = local_tokens // latent_count
    weight_scale = (local_tokens * wide) ** (-0.5)
    rows = up_weight.shape[0]

    ids = jnp.concatenate([codes(labels), codes(timesteps)])
    ids = jnp.pad(ids[None, :], ((0, rows - 1), (0, LANES - ids.shape[0])))
    shard = jnp.concatenate(
        [
            up_weight,
            jnp.transpose(down_weight),
            in_weight.reshape(rows, 3 * width),
            jnp.transpose(out_weight),
            modulation_weight.reshape(rows, 6 * width),
            ids,
        ],
        axis=1,
    )
    bias_parts = [in_bias.reshape(-1), out_bias, up_bias, down_bias, modulation_bias.reshape(-1)]
    biases = jnp.concatenate(bias_parts)
    pad = -biases.shape[0] % (8 * LANES)
    biases = jnp.pad(biases, (0, pad)).reshape(-1, LANES)
    full, tokens, upstream, both = gather_all(wide, shard, latent_tokens, cotangent, biases)
    ids_all = full[0, :, 0, -LANES:].astype(jnp.int32)
    pick = lambda n: ids_all[:, n * latent_count : (n + 1) * latent_count].reshape(-1)
    labels_all = pick(0) * 256 + pick(1)
    times_all = pick(2) * 256 + pick(3)
    class_ids = jnp.arange(class_table.shape[0], dtype=jnp.int32)
    every_hot = (labels_all[:, None] == class_ids[None, :]).astype(bf)
    condition_all = jnp.dot(every_hot, class_table, preferred_element_type=f32) + time_features(
        times_all
    )
    activated_all = jax.nn.silu(condition_all).astype(bf)
    first = me * latent_count + core * own
    condition = lax.dynamic_slice_in_dim(condition_all, first, own, 0)
    activated = lax.dynamic_slice_in_dim(activated_all, first, own, 0)

    full = full.reshape(2, rows * wide, -1)
    flat = both.reshape(2, -1)
    offset = 0
    halves = []
    for part in bias_parts:
        halves.append(flat[:, offset : offset + part.shape[0]])
        offset += part.shape[0]
    bias_in, bias_out, bias_up, bias_down, bias_mod = halves
    mod_at = 2 * hidden + 4 * width
    mod_full = full[:, :, mod_at : mod_at + 6 * width]
    modulation = jnp.einsum("bd,ndf->nbf", activated, mod_full, preferred_element_type=f32) + bias_mod[:, None]
    modulation = jnp.transpose(modulation.reshape(2, own, 6, width), (1, 2, 0, 3)).reshape(own, 6, 2 * width)

    block_output, token_grads, parts, grad_modulation, bias_sums = block_pass(
        tokens.reshape(2 * width, -1), upstream.reshape(2 * width, -1), full, modulation,
        bias_in, bias_out, bias_up, bias_down, own, sequence, width, hidden,
    )

    grad_modulation_bf = grad_modulation.astype(bf)
    by_half = jnp.transpose(grad_modulation_bf.reshape(own, 6, 2, width), (2, 0, 1, 3)).reshape(2, own, 6 * width)
    grad_activated = jnp.einsum("nbf,ndf->bd", by_half, mod_full, preferred_element_type=f32)
    condition_rows = (grad_activated * silu_slope(condition) * sequence ** (-0.5)).astype(bf)
    message = jnp.concatenate(
        [
            by_half.reshape(2, -1),
            jnp.broadcast_to(condition_rows.reshape(1, -1), (2, own * 2 * width)),
            bias_sums.astype(bf),
        ],
        axis=1,
    )
    used = message.shape[1]
    message = jnp.pad(message, ((0, 0), (0, -used % (16 * LANES)))).reshape(2, -1, LANES)
    total, messages, block_half, token_half = scatter_all(
        wide, parts.reshape(2, wide, rows, -1), message, block_output, token_grads
    )
    flat_notes = messages.reshape(wide * 2, -1)
    gm_all = flat_notes[:, : own * 6 * width].reshape(wide * latent_count, 6 * width)
    cond_all = flat_notes[:, own * 6 * width : own * 8 * width].reshape(wide * latent_count, 2 * width)
    sums = jnp.sum(flat_notes[:, own * 8 * width : used].astype(f32), axis=0) * weight_scale
    act_mine = lax.dynamic_slice_in_dim(activated_all, me * rows, rows, 1)
    mod_grads = jnp.einsum("bd,bf->df", act_mine, gm_all, preferred_element_type=f32) * weight_scale
    mod_bias_grads = jnp.sum(gm_all.astype(f32), axis=0) * weight_scale
    table_grads = jnp.einsum("bc,bd->cd", every_hot, cond_all, preferred_element_type=f32)
    condition_grads = lax.dynamic_slice_in_dim(cond_all, me * latent_count, latent_count, 0).astype(f32)
    total = total * weight_scale
    up_part = total[:, :hidden]
    down_part = jnp.transpose(total[:, hidden : 2 * hidden])
    in_part = total[:, 2 * hidden : 2 * hidden + 3 * width].reshape(rows, 3, width)
    out_part = jnp.transpose(total[:, 2 * hidden + 3 * width :])
    return (
        block_half,
        token_half,
        condition_grads,
        table_grads,
        mod_grads.reshape(rows, 6, width),
        mod_bias_grads.reshape(6, width),
        in_part,
        sums[: 2 * width].reshape(2, width),
        out_part,
        sums[2 * width : 3 * width],
        up_part,
        sums[3 * width : 3 * width + hidden],
        down_part,
        sums[3 * width + hidden :],
    )


def solution(mesh):
    return jax.shard_map(
        shards,
        mesh=mesh,
        in_specs=(
            P("narrow", "wide"),
            P("wide"),
            P("wide"),
            P(),
            P("wide", None, "narrow"),
            P(None, "narrow"),
            P("wide", None, "narrow"),
            P(None, "narrow"),
            P("narrow", "wide"),
            P("narrow"),
            P("wide", "narrow"),
            P("narrow"),
            P("narrow", "wide"),
            P("narrow"),
            P("narrow", "wide"),
        ),
        out_specs=(
            P("narrow", "wide"),
            P("narrow", "wide"),
            P("wide", None),
            P(),
            P("wide", None, "narrow"),
            P(None, "narrow"),
            P("wide", None, "narrow"),
            P(None, "narrow"),
            P("narrow", "wide"),
            P("narrow"),
            P("wide", "narrow"),
            P("narrow"),
            P("narrow", "wide"),
            P("narrow"),
        ),
        check_vma=False,
    )
```

```python
import functools
import math

import jax
import jax.numpy as jnp
from jax import lax
from jax.experimental import pallas as pl
from jax.experimental.pallas import tpu as pltpu
from jax.sharding import PartitionSpec as P

D = 384
HD = 64
LANES = 128
MESH = pl.DeviceIdType.MESH
VMEM_LIMIT = 60 * 1024 * 1024


EPS = 1e-06
GELU_K = 0.7978845608028654
GELU_A = 0.044715


def time_features(timesteps):
    half_width = D // 2
    frequencies = jnp.exp(
        jnp.arange(half_width, dtype=jnp.float32) * (-math.log(10000.0) / half_width)
    )
    angles = timesteps.astype(jnp.float32)[:, None] * frequencies[None, :]
    return jnp.concatenate([jnp.cos(angles), jnp.sin(angles)], axis=1)


def gelu_value(inputs):
    inner = GELU_K * (inputs + GELU_A * inputs * inputs * inputs)
    return 0.5 * inputs * (1.0 + jnp.tanh(inner))


def gelu_slope(inputs):
    inner = GELU_K * (inputs + GELU_A * inputs * inputs * inputs)
    tangent = jnp.tanh(inner)
    return 0.5 * (1.0 + tangent) + 0.5 * inputs * (1.0 - tangent * tangent) * GELU_K * (
        1.0 + 3.0 * GELU_A * inputs * inputs
    )


def silu_slope(inputs):
    sigmoid = jax.nn.sigmoid(inputs)
    return sigmoid * (1.0 + inputs * (1.0 - sigmoid))


def plane(wide):
    side = max(1, round((wide / 2) ** (1 / 3)))
    while wide % (side * side):
        side -= 1
    return wide // (side * side), side


class Place:
    def __init__(self, wide):
        self.deep, self.side = plane(wide)
        self.me = lax.axis_index("wide")
        self.core = lax.axis_index("narrow")
        self.z = self.me // (self.side * self.side)
        rest = self.me % (self.side * self.side)
        major, minor = rest // self.side, rest % self.side
        self.p = major + self.core * (minor - major)
        self.q = minor + self.core * (major - minor)
        self.p_stride = self.side + self.core * (1 - self.side)
        self.q_stride = 1 + self.core * (self.side - 1)

    def index(self, dz, dp, dq):
        return (
            ((self.z + dz) % self.deep) * (self.side * self.side)
            + ((self.p + dp) % self.side) * self.p_stride
            + ((self.q + dq) % self.side) * self.q_stride
        )

    def line_peers(self):
        return (
            [self.index(dz, 0, 0) for dz in range(1, self.deep)]
            + [self.index(0, dp, 0) for dp in range(1, self.side)]
            + [self.index(0, 0, dq) for dq in range(1, self.side)]
        )


def gather_kernel(
    wide, shard, tokens, upstream, biases,
    full, tokens_out, upstream_out, biases_out,
    send, recv, pair_send, pair_recv, swap_send, swap_recv, local,
):
    at = Place(wide)
    core, other = at.core, 1 - at.core
    barrier = pltpu.get_barrier_semaphore()
    peers = at.line_peers()
    for peer in peers:
        pl.semaphore_signal(barrier, 1, device_id=(peer, core), device_id_type=MESH)
    pl.semaphore_signal(barrier, 1, device_id=(at.me, other), device_id_type=MESH)
    pl.semaphore_wait(barrier, len(peers) + 1)
    waits = []
    count = 0

    def push(src, block, target):
        nonlocal count
        copy = pltpu.make_async_remote_copy(
            src, full.at[core, block], send.at[count], recv.at[block],
            device_id=(target, core), device_id_type=MESH,
        )
        copy.start()
        waits.append(copy)
        count += 1

    def share(src, block):
        copy = pltpu.make_async_remote_copy(
            src, full.at[core, block], pair_send.at[block], pair_recv.at[block],
            device_id=(at.me, other), device_id_type=MESH,
        )
        copy.start()
        waits.append(copy)

    def arrived(block):
        pltpu.make_async_copy(full.at[core, block], full.at[core, block], recv.at[block]).wait()

    for dz in range(1, at.deep):
        push(shard, at.me, at.index(dz, 0, 0))
    for dp in range(1, at.side):
        push(shard, at.me, at.index(0, dp, 0))
    for dq in range(1, at.side):
        push(shard, at.me, at.index(0, 0, dq))
    share(shard, at.me)
    half = tokens_out.shape[2]
    mine = pl.ds(pl.multiple_of(core * half, LANES), half)
    theirs = pl.ds(pl.multiple_of(other * half, LANES), half)
    for which, (src, dst) in enumerate(
        [(tokens.at[:, theirs], tokens_out), (upstream.at[:, theirs], upstream_out), (biases, biases_out)]
    ):
        copy = pltpu.make_async_remote_copy(
            src, dst.at[core], swap_send.at[which], swap_recv.at[which],
            device_id=(at.me, other), device_id_type=MESH,
        )
        copy.start()
        waits.append(copy)
    keeps = [
        pltpu.make_async_copy(src, dst, local.at[which])
        for which, (src, dst) in enumerate(
            [
                (tokens.at[:, mine], tokens_out.at[core]),
                (upstream.at[:, mine], upstream_out.at[core]),
                (biases, biases_out.at[core]),
                (shard, full.at[core, at.me]),
            ]
        )
    ]
    for keep in keeps:
        keep.start()
    for dz in range(1, at.deep):
        block = at.index(dz, 0, 0)
        arrived(block)
        for dp in range(1, at.side):
            push(full.at[core, block], block, at.index(0, dp, 0))
        for dq in range(1, at.side):
            push(full.at[core, block], block, at.index(0, 0, dq))
        share(full.at[core, block], block)
    for dz in range(at.deep):
        for dp in range(1, at.side):
            block = at.index(dz, dp, 0)
            arrived(block)
            for dq in range(1, at.side):
                push(full.at[core, block], block, at.index(0, 0, dq))
            share(full.at[core, block], block)
    for dz in range(at.deep):
        for dq in range(1, at.side):
            for dp in range(at.side):
                block = at.index(dz, dp, dq)
                arrived(block)
                share(full.at[core, block], block)
    for keep in keeps:
        keep.wait()
    for copy in waits:
        copy.wait_send()
    for block in range(wide):
        pltpu.make_async_copy(full.at[core, block], full.at[core, block], pair_recv.at[block]).wait()
    for which, (src, dst) in enumerate(
        [(tokens_out.at[core], None), (upstream_out.at[core], None), (biases_out.at[core], None)]
    ):
        pltpu.make_async_copy(src, src, swap_recv.at[which]).wait()


def gather_all(wide, shard, tokens, upstream, biases):
    rows, columns = shard.shape
    features, count = tokens.shape
    deep, side = plane(wide)
    sends = wide * (deep + 2 * side)
    vmem = pl.BlockSpec(memory_space=pltpu.VMEM)
    return pl.pallas_call(
        functools.partial(gather_kernel, wide),
        name="gather",
        out_shape=(
            jax.ShapeDtypeStruct((2, wide, rows, columns), shard.dtype),
            jax.ShapeDtypeStruct((2, features, count // 2), tokens.dtype),
            jax.ShapeDtypeStruct((2, features, count // 2), tokens.dtype),
            jax.ShapeDtypeStruct((2,) + biases.shape, biases.dtype),
        ),
        in_specs=[vmem] * 4,
        out_specs=(vmem,) * 4,
        scratch_shapes=[
            pltpu.SemaphoreType.DMA((sends,)),
            pltpu.SemaphoreType.DMA((wide,)),
            pltpu.SemaphoreType.DMA((wide,)),
            pltpu.SemaphoreType.DMA((wide,)),
            pltpu.SemaphoreType.DMA((3,)),
            pltpu.SemaphoreType.DMA((3,)),
            pltpu.SemaphoreType.DMA((4,)),
        ],
        compiler_params=pltpu.CompilerParams(
            collective_id=0, has_side_effects=True, vmem_limit_bytes=VMEM_LIMIT
        ),
    )(shard, tokens, upstream, biases)


def scatter_kernel(
    wide, parts, message, block_out, token_out,
    total, messages, block_half, token_half,
    from_pair, from_q, from_p, from_z, sums,
    send, pair_send, pair_recv, q_recv, p_recv, z_recv,
    note_send, note_recv, swap_send, swap_recv, local,
):
    at = Place(wide)
    core, other = at.core, 1 - at.core
    barrier = pltpu.get_barrier_semaphore()
    for step in range(wide):
        peer = (at.me + step) % wide
        if step:
            pl.semaphore_signal(barrier, 1, device_id=(peer, core), device_id_type=MESH)
        pl.semaphore_signal(barrier, 1, device_id=(peer, other), device_id_type=MESH)
    pl.semaphore_wait(barrier, 2 * wide - 1)
    waits = []

    deep, side = at.deep, at.side
    order = (
        [(dz, dp, dq) for dq in range(1, side) for dp in range(side) for dz in range(deep)]
        + [(dz, dp, 0) for dp in range(1, side) for dz in range(deep)]
        + [(dz, 0, 0) for dz in range(1, deep)]
        + [(0, 0, 0)]
    )
    for dz, dp, dq in order:
        block = at.index(dz, dp, dq)
        copy = pltpu.make_async_remote_copy(
            parts.at[other, block], from_pair.at[block], pair_send.at[block], pair_recv.at[block],
            device_id=(at.me, other), device_id_type=MESH,
        )
        copy.start()
        waits.append(copy)
    for step in range(wide):
        peer = (at.me + step) % wide
        for flip in range(2):
            if step == 0 and flip == 0:
                continue
            seat = core if flip == 0 else other
            copy = pltpu.make_async_remote_copy(
                message.at[seat], messages.at[at.me, core],
                note_send.at[step, flip], note_recv.at[at.me, core],
                device_id=(peer, seat), device_id_type=MESH,
            )
            copy.start()
            waits.append(copy)
    half = block_out.shape[0] // 2
    span = block_out.shape[1]
    columns = pl.ds(pl.multiple_of(core * span, LANES), span)
    mine = pl.ds(pl.multiple_of(core * half, 8), half)
    theirs = pl.ds(pl.multiple_of(other * half, 8), half)
    keeps = [pltpu.make_async_copy(message.at[core], messages.at[at.me, core], local.at[2])]
    for which, (src, dst) in enumerate([(block_out, block_half), (token_out, token_half)]):
        copy = pltpu.make_async_remote_copy(
            src.at[theirs], dst.at[:, columns], swap_send.at[which], swap_recv.at[which],
            device_id=(at.me, other), device_id_type=MESH,
        )
        copy.start()
        waits.append(copy)
        keeps.append(pltpu.make_async_copy(src.at[mine], dst.at[:, columns], local.at[which]))
    for keep in keeps:
        keep.start()

    def landed(ref, sem):
        pltpu.make_async_copy(ref, ref, sem).wait()

    f32 = jnp.float32
    for number, (dz, dp, dq) in enumerate(order):
        block = at.index(dz, dp, dq)
        landed(from_pair.at[block], pair_recv.at[block])
        value = parts[core, block].astype(f32) + from_pair[block].astype(f32)
        zs, ps = (at.z + dz) % deep, (at.p + dp) % side
        if dq == 0:
            for s in range(side - 1):
                landed(from_q.at[s, zs, ps], q_recv.at[s, zs, ps])
                value += from_q[s, zs, ps].astype(f32)
            if dp == 0:
                for s in range(side - 1):
                    landed(from_p.at[s, zs], p_recv.at[s, zs])
                    value += from_p[s, zs].astype(f32)
        if dq:
            target, slot, sem = (
                at.index(0, 0, dq), from_q.at[side - 1 - dq, zs, ps], q_recv.at[side - 1 - dq, zs, ps]
            )
        elif dp:
            target, slot, sem = (
                at.index(0, dp, 0), from_p.at[side - 1 - dp, zs], p_recv.at[side - 1 - dp, zs]
            )
        elif dz:
            target, slot, sem = at.index(dz, 0, 0), from_z.at[deep - 1 - dz], z_recv.at[deep - 1 - dz]
        else:
            for s in range(deep - 1):
                landed(from_z.at[s], z_recv.at[s])
                value += from_z[s].astype(f32)
            total[...] = value
            continue
        sums[block] = value.astype(jnp.bfloat16)
        copy = pltpu.make_async_remote_copy(
            sums.at[block], slot, send.at[number], sem,
            device_id=(target, core), device_id_type=MESH,
        )
        copy.start()
        waits.append(copy)
    for keep in keeps:
        keep.wait()
    for copy in waits:
        copy.wait_send()
    for step in range(wide):
        peer = (at.me + step) % wide
        if step:
            landed(messages.at[peer, core], note_recv.at[peer, core])
        landed(messages.at[peer, other], note_recv.at[peer, other])
    spare = pl.ds(pl.multiple_of(other * span, LANES), span)
    landed(block_half.at[:, spare], swap_recv.at[0])
    landed(token_half.at[:, spare], swap_recv.at[1])


def scatter_all(wide, parts, message, block_out, token_out):
    rows, columns = parts.shape[2:]
    features, count = block_out.shape
    deep, side = plane(wide)
    vmem = pl.BlockSpec(memory_space=pltpu.VMEM)
    bf, f32 = jnp.bfloat16, jnp.float32
    dma = pltpu.SemaphoreType.DMA
    return pl.pallas_call(
        functools.partial(scatter_kernel, wide),
        name="scatter",
        out_shape=(
            jax.ShapeDtypeStruct((rows, columns), f32),
            jax.ShapeDtypeStruct((wide,) + message.shape, bf),
            jax.ShapeDtypeStruct((features // 2, 2 * count), f32),
            jax.ShapeDtypeStruct((features // 2, 2 * count), f32),
        ),
        in_specs=[vmem] * 4,
        out_specs=(vmem,) * 4,
        scratch_shapes=[
            pltpu.VMEM((wide, rows, columns), bf),
            pltpu.VMEM((max(side - 1, 1), deep, side, rows, columns), bf),
            pltpu.VMEM((max(side - 1, 1), deep, rows, columns), bf),
            pltpu.VMEM((max(deep - 1, 1), rows, columns), bf),
            pltpu.VMEM((wide, rows, columns), bf),
            dma((wide,)),
            dma((wide,)),
            dma((wide,)),
            dma((max(side - 1, 1), deep, side)),
            dma((max(side - 1, 1), deep)),
            dma((max(deep - 1, 1),)),
            dma((wide, 2)),
            dma((wide, 2)),
            dma((2,)),
            dma((2,)),
            dma((3,)),
        ],
        compiler_params=pltpu.CompilerParams(
            collective_id=1, has_side_effects=True, vmem_limit_bytes=VMEM_LIMIT
        ),
    )(parts, message, block_out, token_out)


def norm_forward(values):
    average = jnp.mean(values, axis=-1, keepdims=True)
    centred = values - average
    inv_std = lax.rsqrt(jnp.mean(centred * centred, axis=-1, keepdims=True) + EPS)
    return centred * inv_std, inv_std


def norm_backward(grad_norm, normed, inv_std):
    first = jnp.mean(grad_norm, axis=-1, keepdims=True)
    second = jnp.mean(grad_norm * normed, axis=-1, keepdims=True)
    return inv_std * (grad_norm - first - normed * second)


def block_kernel(
    own, sequence, width, hidden,
    tokens, upstream, full, modulation, bias_in, bias_out, bias_up, bias_down,
    block_out, token_out, parts, grad_mod, sum_heads, sum_out, sum_up, sum_down,
    hid, upg, normed, inv, mod_bf, normed_two, inv_two, mod_two, gff, attention, feed, gmod,
    qkv, att_heads, att, weights, gatt_heads, gatt, gproj_heads, gproj,
):
    bf, f32 = jnp.bfloat16, jnp.float32
    features = 2 * width
    heads = features // HD
    per_half = heads // 2
    count = own * sequence
    score_scale = HD ** (-0.5)
    rows = LANES if sequence % LANES == 0 else sequence
    blocks = count // rows
    chunk = 256 if hidden % 256 == 0 else hidden
    chunks = hidden // chunk
    in_at, out_at = 2 * hidden, 2 * hidden + 3 * width

    def dot(a, b, left, right):
        return lax.dot_general(a, b, (((left,), (right,)), ((), ())), preferred_element_type=f32)

    def total(value):
        return jnp.sum(value, axis=0, keepdims=True)

    grad_mod[...] = jnp.zeros_like(grad_mod)
    sum_heads[...] = jnp.zeros_like(sum_heads)
    sum_out[...] = jnp.zeros_like(sum_out)
    sum_down[...] = jnp.zeros_like(sum_down)
    feed[...] = jnp.zeros_like(feed)
    gmod[...] = jnp.zeros_like(gmod)

    def span(r):
        return pl.ds(pl.multiple_of(r * rows, rows), rows), (r * rows) // sequence

    @pl.loop(0, blocks)
    def _(r):
        at, b = span(r)
        values = jnp.transpose(tokens[:, at])
        hid[at, :] = values
        unit, scale = norm_forward(values)
        normed[at, :] = unit
        inv[at, :] = scale
        mod_bf[at, :] = (unit * (1.0 + modulation[b, 1:2, :]) + modulation[b, 0:1, :]).astype(bf)
        up = jnp.transpose(upstream[:, at])
        upg[at, :] = up
        grad = modulation[b, 5:6, :] * up
        gff[at, :] = grad.astype(bf)
        sum_down[...] += total(grad)

    @pl.loop(0, blocks)
    def _(r):
        at, b = span(r)
        for n in range(2):
            out = dot(mod_bf[at, :], full[n, :, in_at:out_at], 1, 0)
            for j in range(3):
                for h in range(per_half):
                    low = j * width + h * HD
                    piece = out[:, low : low + HD]
                    if j != 1:
                        piece = piece + bias_in[j // 2, n * per_half + h]
                    qkv[j, n * per_half + h, at, :] = piece.astype(bf)

    @pl.loop(0, own * heads)
    def _(i):
        b, h = i // heads, i % heads
        at = pl.ds(pl.multiple_of(b * sequence, sequence), sequence)
        scores = dot(qkv[0, h, at, :], qkv[1, h, at, :], 1, 1) * score_scale
        log_total = jnp.log(jnp.sum(jnp.exp(scores), axis=-1, keepdims=True))
        mix = jnp.exp(scores - log_total)
        weights[i] = mix
        att_heads[h, at, :] = dot(mix.astype(bf), qkv[2, h, at, :], 1, 0).astype(bf)

    for n in range(2):
        att[n] = jnp.concatenate([att_heads[n * per_half + h] for h in range(per_half)], axis=1)

    @pl.loop(0, blocks)
    def _(r):
        at, b = span(r)
        result = bias_out[...] + sum(
            dot(att[n, at, :], full[n, :, out_at : out_at + width], 1, 1) for n in range(2)
        )
        attention[at, :] = result
        middle = hid[at, :] + modulation[b, 2:3, :] * result
        hid[at, :] = middle
        unit, scale = norm_forward(middle)
        normed_two[at, :] = unit
        inv_two[at, :] = scale
        mod_two[at, :] = (unit * (1.0 + modulation[b, 4:5, :]) + modulation[b, 3:4, :]).astype(bf)

    @pl.loop(0, 2 * chunks)
    def _(i):
        n, c = i // chunks, i % chunks
        at = pl.ds(pl.multiple_of(c * chunk, chunk), chunk)
        down_at = pl.ds(pl.multiple_of(hidden + c * chunk, chunk), chunk)
        up_w, down_w = full[n, :, at], full[n, :, down_at]
        pre = dot(mod_two[...], up_w, 1, 0) + bias_up[n, :, at]
        tangent = jnp.tanh(GELU_K * (pre + GELU_A * pre * pre * pre))
        act = (0.5 * pre * (1.0 + tangent)).astype(bf)
        slope = 0.5 * (1.0 + tangent) + 0.5 * pre * (1.0 - tangent * tangent) * GELU_K * (
            1.0 + 3.0 * GELU_A * pre * pre
        )
        feed[...] += dot(act, down_w, 1, 1)
        parts[n, :, down_at] = dot(gff[...], act, 0, 0).astype(bf)
        grad = dot(gff[...], down_w, 1, 0) * slope
        sum_up[n, :, at] = total(grad)
        grad_bf = grad.astype(bf)
        parts[n, :, at] = dot(mod_two[...], grad_bf, 0, 0).astype(bf)
        gmod[...] += dot(grad_bf, up_w, 1, 1)

    @pl.loop(0, blocks)
    def _(r):
        at, b = span(r)
        ff = feed[at, :] + bias_down[...]
        up = upg[at, :]
        block_out[:, at] = jnp.transpose(hid[at, :] + modulation[b, 5:6, :] * ff)
        grad_mod[b, 5:6, :] += total(up * ff)
        grad, unit = gmod[at, :], normed_two[at, :]
        grad_mod[b, 3:4, :] += total(grad)
        grad_mod[b, 4:5, :] += total(grad * unit)
        middle = up + norm_backward(grad * (1.0 + modulation[b, 4:5, :]), unit, inv_two[at, :])
        upg[at, :] = middle
        grad_mod[b, 2:3, :] += total(middle * attention[at, :])
        grad_att = modulation[b, 2:3, :] * middle
        sum_out[...] += total(grad_att)
        grad_bf = grad_att.astype(bf)
        gatt[at, :] = grad_bf
        for n in range(2):
            out = dot(grad_bf, full[n, :, out_at : out_at + width], 1, 0).astype(bf)
            for h in range(per_half):
                gatt_heads[n * per_half + h, at, :] = out[:, h * HD : (h + 1) * HD]

    @pl.loop(0, own * heads)
    def _(i):
        b, h = i // heads, i % heads
        at = pl.ds(pl.multiple_of(b * sequence, sequence), sequence)
        mix, grad_out = weights[i], gatt_heads[h, at, :]
        grad_mix = dot(grad_out, qkv[2, h, at, :], 1, 1)
        dots = jnp.sum(mix * grad_mix, axis=-1, keepdims=True)
        grad_scores = (mix * (grad_mix - dots) * score_scale).astype(bf)
        grad_q = dot(grad_scores, qkv[1, h, at, :], 1, 0)
        grad_k = dot(grad_scores, qkv[0, h, at, :], 0, 0)
        grad_v = dot(mix.astype(bf), grad_out, 0, 0)
        gproj_heads[0, h, at, :] = grad_q.astype(bf)
        gproj_heads[1, h, at, :] = grad_k.astype(bf)
        gproj_heads[2, h, at, :] = grad_v.astype(bf)
        sum_heads[0, h] += total(grad_q)
        sum_heads[1, h] += total(grad_v)

    for n in range(2):
        gproj[n] = jnp.concatenate(
            [gproj_heads[j, n * per_half + h] for j in range(3) for h in range(per_half)], axis=1
        )
        parts[n, :, in_at:] = jnp.concatenate(
            [dot(mod_bf[...], gproj[n], 0, 0), dot(gatt[...], att[n], 0, 0)], axis=1
        ).astype(bf)

    @pl.loop(0, blocks)
    def _(r):
        at, b = span(r)
        grad = sum(dot(gproj[n, at, :], full[n, :, in_at:out_at], 1, 1) for n in range(2))
        unit = normed[at, :]
        grad_mod[b, 0:1, :] += total(grad)
        grad_mod[b, 1:2, :] += total(grad * unit)
        back = norm_backward(grad * (1.0 + modulation[b, 1:2, :]), unit, inv[at, :])
        token_out[:, at] = jnp.transpose(upg[at, :] + back)


def block_pass(
    tokens, upstream, full, modulation, bias_in, bias_out, bias_up, bias_down, own, sequence, width, hidden
):
    bf, f32 = jnp.bfloat16, jnp.float32
    features = 2 * width
    heads = features // HD
    count = own * sequence
    bias_in = jnp.transpose(bias_in.reshape(2, 2, width), (1, 0, 2)).reshape(2, heads, 1, HD)
    vmem = pl.BlockSpec(memory_space=pltpu.VMEM)
    sds = jax.ShapeDtypeStruct
    wide_f32, wide_bf = pltpu.VMEM((count, features), f32), pltpu.VMEM((count, features), bf)
    column = pltpu.VMEM((count, 1), f32)
    by_head = pltpu.VMEM((heads, count, HD), bf)
    by_head_three = pltpu.VMEM((3, heads, count, HD), bf)
    block_out, token_out, parts, grad_mod, sum_heads, sum_out, sum_up, sum_down = pl.pallas_call(
        functools.partial(block_kernel, own, sequence, width, hidden),
        name="block",
        out_shape=(
            sds((features, count), f32),
            sds((features, count), f32),
            sds((2, features, 2 * hidden + 4 * width), bf),
            sds((own, 6, features), f32),
            sds((2, heads, 1, HD), f32),
            sds((1, features), f32),
            sds((2, 1, hidden), f32),
            sds((1, features), f32),
        ),
        in_specs=[vmem] * 8,
        out_specs=(vmem,) * 8,
        scratch_shapes=[
            wide_f32, wide_f32, wide_f32, column, wide_bf, wide_f32, column, wide_bf, wide_bf, wide_f32,
            wide_f32, wide_f32,
            by_head_three, by_head, pltpu.VMEM((2, count, width), bf),
            pltpu.VMEM((own * heads, sequence, sequence), f32),
            by_head, wide_bf, by_head_three, pltpu.VMEM((2, count, 3 * width), bf),
        ],
        compiler_params=pltpu.CompilerParams(vmem_limit_bytes=VMEM_LIMIT),
    )(
        tokens, upstream, full, modulation, bias_in, bias_out.reshape(1, -1),
        bias_up.reshape(2, 1, hidden), bias_down.reshape(1, -1),
    )
    by_half = lambda value: value.reshape(2, -1)
    bias_sums = jnp.concatenate(
        [
            by_half(sum_heads[0]), by_half(sum_heads[1]), by_half(sum_out), by_half(sum_up), by_half(sum_down),
        ],
        axis=1,
    )
    return block_out, token_out, parts, grad_mod, bias_sums


def codes(values):
    return jnp.concatenate([values // 256, values % 256]).astype(jnp.bfloat16)


def shards(
    latent_tokens,
    labels,
    timesteps,
    class_table,
    modulation_weight,
    modulation_bias,
    in_weight,
    in_bias,
    out_weight,
    out_bias,
    up_weight,
    up_bias,
    down_weight,
    down_bias,
    cotangent,
):
    bf, f32 = jnp.bfloat16, jnp.float32
    wide = lax.axis_size("wide")
    me, core = lax.axis_index("wide"), lax.axis_index("narrow")
    latent_count = labels.shape[0]
    own = latent_count // 2
    width = latent_tokens.shape[0]
    hidden = up_weight.shape[1]
    local_tokens = latent_tokens.shape[1]
    sequence = local_tokens // latent_count
    weight_scale = (local_tokens * wide) ** (-0.5)
    rows = up_weight.shape[0]

    ids = jnp.concatenate([codes(labels), codes(timesteps)])
    ids = jnp.pad(ids[None, :], ((0, rows - 1), (0, LANES - ids.shape[0])))
    shard = jnp.concatenate(
        [
            up_weight,
            jnp.transpose(down_weight),
            in_weight.reshape(rows, 3 * width),
            jnp.transpose(out_weight),
            modulation_weight.reshape(rows, 6 * width),
            ids,
        ],
        axis=1,
    )
    bias_parts = [in_bias.reshape(-1), out_bias, up_bias, down_bias, modulation_bias.reshape(-1)]
    biases = jnp.concatenate(bias_parts)
    pad = -biases.shape[0] % (8 * LANES)
    biases = jnp.pad(biases, (0, pad)).reshape(-1, LANES)
    full, tokens, upstream, both = gather_all(wide, shard, latent_tokens, cotangent, biases)
    ids_all = full[0, :, 0, -LANES:].astype(jnp.int32)
    pick = lambda n: ids_all[:, n * latent_count : (n + 1) * latent_count].reshape(-1)
    labels_all = pick(0) * 256 + pick(1)
    times_all = pick(2) * 256 + pick(3)
    class_ids = jnp.arange(class_table.shape[0], dtype=jnp.int32)
    every_hot = (labels_all[:, None] == class_ids[None, :]).astype(bf)
    condition_all = jnp.dot(every_hot, class_table, preferred_element_type=f32) + time_features(
        times_all
    )
    activated_all = jax.nn.silu(condition_all).astype(bf)
    first = me * latent_count + core * own
    condition = lax.dynamic_slice_in_dim(condition_all, first, own, 0)
    activated = lax.dynamic_slice_in_dim(activated_all, first, own, 0)

    full = full.reshape(2, rows * wide, -1)
    flat = both.reshape(2, -1)
    offset = 0
    halves = []
    for part in bias_parts:
        halves.append(flat[:, offset : offset + part.shape[0]])
        offset += part.shape[0]
    bias_in, bias_out, bias_up, bias_down, bias_mod = halves
    mod_at = 2 * hidden + 4 * width
    mod_full = full[:, :, mod_at : mod_at + 6 * width]
    modulation = jnp.einsum("bd,ndf->nbf", activated, mod_full, preferred_element_type=f32) + bias_mod[:, None]
    modulation = jnp.transpose(modulation.reshape(2, own, 6, width), (1, 2, 0, 3)).reshape(own, 6, 2 * width)

    block_output, token_grads, parts, grad_modulation, bias_sums = block_pass(
        tokens.reshape(2 * width, -1), upstream.reshape(2 * width, -1), full, modulation,
        bias_in, bias_out, bias_up, bias_down, own, sequence, width, hidden,
    )

    grad_modulation_bf = grad_modulation.astype(bf)
    by_half = jnp.transpose(grad_modulation_bf.reshape(own, 6, 2, width), (2, 0, 1, 3)).reshape(2, own, 6 * width)
    grad_activated = jnp.einsum("nbf,ndf->bd", by_half, mod_full, preferred_element_type=f32)
    condition_rows = (grad_activated * silu_slope(condition) * sequence ** (-0.5)).astype(bf)
    message = jnp.concatenate(
        [
            by_half.reshape(2, -1),
            jnp.broadcast_to(condition_rows.reshape(1, -1), (2, own * 2 * width)),
            bias_sums.astype(bf),
        ],
        axis=1,
    )
    used = message.shape[1]
    message = jnp.pad(message, ((0, 0), (0, -used % (16 * LANES)))).reshape(2, -1, LANES)
    total, messages, block_half, token_half = scatter_all(
        wide, parts.reshape(2, wide, rows, -1), message, block_output, token_grads
    )
    flat_notes = messages.reshape(wide * 2, -1)
    gm_all = flat_notes[:, : own * 6 * width].reshape(wide * latent_count, 6 * width)
    cond_all = flat_notes[:, own * 6 * width : own * 8 * width].reshape(wide * latent_count, 2 * width)
    sums = jnp.sum(flat_notes[:, own * 8 * width : used].astype(f32), axis=0) * weight_scale
    act_mine = lax.dynamic_slice_in_dim(activated_all, me * rows, rows, 1)
    mod_grads = jnp.einsum("bd,bf->df", act_mine, gm_all, preferred_element_type=f32) * weight_scale
    mod_bias_grads = jnp.sum(gm_all.astype(f32), axis=0) * weight_scale
    table_grads = jnp.einsum("bc,bd->cd", every_hot, cond_all, preferred_element_type=f32)
    condition_grads = lax.dynamic_slice_in_dim(cond_all, me * latent_count, latent_count, 0).astype(f32)
    total = total * weight_scale
    up_part = total[:, :hidden]
    down_part = jnp.transpose(total[:, hidden : 2 * hidden])
    in_part = total[:, 2 * hidden : 2 * hidden + 3 * width].reshape(rows, 3, width)
    out_part = jnp.transpose(total[:, 2 * hidden + 3 * width :])
    return (
        block_half,
        token_half,
        condition_grads,
        table_grads,
        mod_grads.reshape(rows, 6, width),
        mod_bias_grads.reshape(6, width),
        in_part,
        sums[: 2 * width].reshape(2, width),
        out_part,
        sums[2 * width : 3 * width],
        up_part,
        sums[3 * width : 3 * width + hidden],
        down_part,
        sums[3 * width + hidden :],
    )


def solution(mesh):
    return jax.shard_map(
        shards,
        mesh=mesh,
        in_specs=(
            P("narrow", "wide"),
            P("wide"),
            P("wide"),
            P(),
            P("wide", None, "narrow"),
            P(None, "narrow"),
            P("wide", None, "narrow"),
            P(None, "narrow"),
            P("narrow", "wide"),
            P("narrow"),
            P("wide", "narrow"),
            P("narrow"),
            P("narrow", "wide"),
            P("narrow"),
            P("narrow", "wide"),
        ),
        out_specs=(
            P("narrow", "wide"),
            P("narrow", "wide"),
            P("wide", None),
            P(),
            P("wide", None, "narrow"),
            P(None, "narrow"),
            P("wide", None, "narrow"),
            P(None, "narrow"),
            P("narrow", "wide"),
            P("narrow"),
            P("wide", "narrow"),
            P("narrow"),
            P("narrow", "wide"),
            P("narrow"),
        ),
        check_vma=False,
    )
```
